32 devices in a mesh: groups: 2 (over y), lon: 4 (over z), lat: 2 (over x), head: 2 (over core).
Axes of the slice: x: 2, y: 2, z: 4, core: 2. Of those that a mesh axis runs over, the one named last changes fastest.
Arguments:
- queries: bfloat16 [4, 4, 128, 1536], P(('groups', 'lat'), 'lon', None, 'head'), parts along dimension 0, may hold values from -12 to 12
- key_tokens: bfloat16 [4, 4, 128, 1536], P(('groups', 'lat'), 'lon', None, 'head'), parts along dimension 0, may hold values from -4 to 4
- value_tokens: bfloat16 [4, 4, 128, 1536], P(('groups', 'lat'), 'lon', None, 'head'), parts along dimension 0, may hold values from -6 to 6
- out_grad: bfloat16 [4, 4, 128, 1536], P(('groups', 'lat'), 'lon', None, 'head'), parts along dimension 0, may hold values from -6 to 6
- counts: int32 [4, 4], P('groups'), parts along dimension 0, may hold values from 16 to 128, as said below
Outputs:
- attended: bfloat16 [4, 4, 128, 1536], P(('groups', 'lat'), 'lon', None, 'head'), parts along dimension 0
- query_grad: bfloat16 [4, 4, 128, 1536], P(('groups', 'lat'), 'lon', None, 'head'), parts along dimension 0
- key_grad: bfloat16 [4, 4, 128, 1536], P(('groups', 'lat'), 'lon', None, 'head'), parts along dimension 0
- value_grad: bfloat16 [4, 4, 128, 1536], P(('groups', 'lat'), 'lon', None, 'head'), parts along dimension 0
The draws below stay inside these ranges and needn't reach their ends.
There are 2 independent parts, one for each index of `groups`. The reference program is written for one: setup_inputs(seed, part) draws one part's arguments, and reference() takes and returns one part's arrays. A program takes and returns all parts, laid end to end along the dimension named above; each array names one. Nothing has to cross between parts.
Inputs may be any that keep to these rules, and one draw needn't show every extreme that they name: `counts`: every row of tiles holds a tile of 128 valid tokens; tiles of the first and last rows hold at least 16 valid tokens, the others at least 64.
All inputs are finite; a program needn't handle non-finite values.
Results may differ from the reference program's by a relative error of at most 0.012.
The reference program's roundings to bfloat16 on the way (of `weights_low` and `grad_scores`) count: a program that leaves them out, or rounds other values in their place, can miss the bound.
Values may be sent and summed in bfloat16 or wider, within the bound.
A program may use at most 64 MiB of HBM per device.

```python
import math
import jax
import jax.numpy as jnp
from jax import lax

HEADS = 12
HD = 128
TILE = 128
LAT_TILES = 2
LON_TILES = 4
WIDTH = 1536


def draw_queries(key, part):
    arr_shape = (LAT_TILES, LON_TILES, TILE, WIDTH)
    base_draw = jnp.clip(2.0 * jax.random.normal(jax.random.fold_in(key, 1), arr_shape, jnp.float32), -12.0, 12.0)
    return base_draw.astype(jnp.bfloat16)


def draw_key_tokens(key, part):
    arr_shape = (LAT_TILES, LON_TILES, TILE, WIDTH)
    base_draw = jnp.clip(jax.random.normal(jax.random.fold_in(key, 2), arr_shape, jnp.float32), -4.0, 4.0)
    return base_draw.astype(jnp.bfloat16)


def draw_counts(key, part):
    row_ids = jnp.arange(LAT_TILES).reshape(LAT_TILES, 1)
    polar_row = (row_ids == 0) | (row_ids == LAT_TILES - 1)
    lowest = jnp.where(polar_row, TILE // 8, TILE // 2)
    raw_bits = jax.random.randint(jax.random.fold_in(key, 3), (LAT_TILES, LON_TILES), 0, 1 << 20)
    drawn_counts = lowest + raw_bits % (TILE + 1 - lowest)
    full_col = jax.random.randint(jax.random.fold_in(key, 4), (LAT_TILES, 1), 0, LON_TILES)
    col_ids = jnp.arange(LON_TILES).reshape(1, LON_TILES)
    return jnp.where(col_ids == full_col, TILE, drawn_counts).astype(jnp.int32)


def block_levels(own_key, dims, shards, least, top_value):
    gain = 1.0
    for dim, parts in shards:
        steps = jax.random.uniform(jax.random.fold_in(jax.random.fold_in(own_key, 6), dim), (parts,), jnp.float32, least / len(shards), top_value / len(shards))
        gain = gain * jnp.repeat(jnp.exp(steps), dims[dim] // parts).reshape((-1,) + (1,) * (len(dims) - 1 - dim))
    return gain


def bell_draw(key, dims, deviation, reach, cuts=(), kind=jnp.bfloat16):
    result = jax.random.normal(key, dims, jnp.float32) * deviation
    if len(cuts) > 0:
        result = block_levels(key, dims, cuts, -0.22, 0.18) * result
    return jnp.clip(result, min=-reach, max=reach).astype(kind)


def setup_inputs(seed: int = 0, part: int = 0) -> dict:
    keys = jax.random.split(jax.random.key(seed), 6)
    part_splits = jax.random.split(jax.random.fold_in(keys[5], part), 6)
    return {
        "queries": draw_queries(jax.random.fold_in(jax.random.fold_in(keys[5], part), 71), part),
        "key_tokens": draw_key_tokens(jax.random.fold_in(jax.random.fold_in(keys[5], part), 71), part),
        "value_tokens": bell_draw(part_splits[2], (LAT_TILES, LON_TILES, TILE, WIDTH), 1.0, 6.0, ((0, 2), (1, 4), (3, 2))),
        "out_grad": bell_draw(part_splits[3], (LAT_TILES, LON_TILES, TILE, WIDTH), 1.0, 6.0, ((0, 2), (1, 4), (3, 2))),
        "counts": draw_counts(jax.random.fold_in(jax.random.fold_in(keys[5], part), 71), part),
    }


def neighbour_tiles(row_at, col_at):
    row_step = jnp.array([-1, -1, -1, 0, 0, 0, 1, 1, 1], dtype=jnp.int32)
    col_step = jnp.array([-1, 0, 1, -1, 0, 1, -1, 0, 1], dtype=jnp.int32)
    row_next = row_at + row_step
    across = (row_next < 0) | (row_next > LAT_TILES - 1)
    col_next = (col_at + col_step + jnp.where(across, LON_TILES // 2, 0)) % LON_TILES
    row_next = jnp.clip(row_next, 0, LAT_TILES - 1)
    return (row_next * LON_TILES + col_next).astype(jnp.int32)

def reference(queries, key_tokens, value_tokens, out_grad, counts):
    tile_count = LAT_TILES * LON_TILES
    flat_q = queries.reshape(tile_count, TILE, HEADS, HD).astype(jnp.float32)
    flat_k = key_tokens.reshape(tile_count, TILE, HEADS, HD).astype(jnp.float32)
    flat_v = value_tokens.reshape(tile_count, TILE, HEADS, HD).astype(jnp.float32)
    flat_g = out_grad.reshape(tile_count, TILE, HEADS, HD).astype(jnp.float32)
    flat_counts = counts.reshape(-1)
    positions = jnp.arange(TILE, dtype=jnp.int32)
    score_scale = 1.0 / math.sqrt(HD)

    def query_tile(index):
        slot_ids = neighbour_tiles(index // LON_TILES, index % LON_TILES)
        key_valid = (positions[None, :] < flat_counts[slot_ids][:, None]).reshape(-1)
        near_keys = flat_k[slot_ids].reshape(9 * TILE, HEADS, HD)
        near_values = flat_v[slot_ids].reshape(9 * TILE, HEADS, HD)
        query_here = flat_q[index]
        grad_here = flat_g[index]
        scores = jnp.einsum('thd,khd->htk', query_here, near_keys) * score_scale
        row_max = lax.optimization_barrier(jnp.max(jnp.where(key_valid, scores, -1e+30), axis=-1, keepdims=True))
        row_total = lax.optimization_barrier(jnp.sum(jnp.where(key_valid, jnp.exp(scores - row_max), 0.0), axis=-1, keepdims=True))
        log_total = row_max + jnp.log(row_total)
        weights = jnp.where(key_valid, jnp.exp(scores - log_total), 0.0)
        weights_low = lax.optimization_barrier(weights.astype(jnp.bfloat16))
        head_out = jnp.einsum('htk,khd->thd', weights_low.astype(jnp.float32), near_values).astype(jnp.bfloat16)
        head_out = lax.optimization_barrier(head_out)
        out_dot = jnp.einsum('thd,thd->ht', grad_here, head_out.astype(jnp.float32))
        grad_weights = jnp.einsum('thd,khd->htk', grad_here, near_values)
        grad_scores = lax.optimization_barrier((weights * (grad_weights - out_dot[:, :, None])).astype(jnp.bfloat16))
        query_part = (jnp.einsum('htk,khd->thd', grad_scores.astype(jnp.float32), near_keys) * score_scale).astype(jnp.bfloat16)
        return (head_out, query_part, log_total[:, :, 0], out_dot)
    tile_ids = jnp.arange(tile_count, dtype=jnp.int32)
    attended, query_grad, log_totals, out_dots = lax.map(query_tile, tile_ids)

    def key_tile(index):
        slot_ids = neighbour_tiles(index // LON_TILES, index % LON_TILES)
        near_q = flat_q[slot_ids].reshape(9 * TILE, HEADS, HD)
        near_g = flat_g[slot_ids].reshape(9 * TILE, HEADS, HD)
        near_total = jnp.transpose(log_totals[slot_ids], (1, 0, 2)).reshape(HEADS, 9 * TILE)
        near_dot = jnp.transpose(out_dots[slot_ids], (1, 0, 2)).reshape(HEADS, 9 * TILE)
        own_valid = positions < flat_counts[index]
        keys_here = flat_k[index]
        values_here = flat_v[index]
        scores = jnp.einsum('qhd,khd->hqk', near_q, keys_here) * score_scale
        weights = jnp.where(own_valid[None, None, :], jnp.exp(scores - near_total[:, :, None]), 0.0)
        weights_low = lax.optimization_barrier(weights.astype(jnp.bfloat16))
        value_part = jnp.einsum('hqk,qhd->khd', weights_low.astype(jnp.float32), near_g).astype(jnp.bfloat16)
        grad_weights = jnp.einsum('qhd,khd->hqk', near_g, values_here)
        grad_scores = lax.optimization_barrier((weights * (grad_weights - near_dot[:, :, None])).astype(jnp.bfloat16))
        key_part = (jnp.einsum('hqk,qhd->khd', grad_scores.astype(jnp.float32), near_q) * score_scale).astype(jnp.bfloat16)
        return (key_part, value_part)
    key_grad, value_grad = lax.map(key_tile, tile_ids)
    full_shape = (LAT_TILES, LON_TILES, TILE, HEADS * HD)
    return (attended.reshape(full_shape), query_grad.reshape(full_shape), key_grad.reshape(full_shape), value_grad.reshape(full_shape))
```

```python
import math

import jax
import jax.numpy as jnp
from jax import lax
from jax.experimental import pallas as pl
from jax.experimental.pallas import tpu as pltpu
from jax.sharding import PartitionSpec as P

HD = 128
LOG2E = 1.4426950408889634


def with_halo(cells, sides, width, closed):
    for axis, dim in sides:
        count = lax.axis_size(axis)
        ends = count if closed else count - 1
        head = lax.slice_in_dim(cells, 0, width, axis=dim)
        tail = lax.slice_in_dim(cells, cells.shape[dim] - width, cells.shape[dim], axis=dim)
        cells = jnp.concatenate(
            [
                lax.ppermute(tail, axis, [(i, (i + 1) % count) for i in range(ends)]),
                cells,
                lax.ppermute(head, axis, [((i + 1) % count, i) for i in range(ends)]),
            ],
            axis=dim,
        )
    return cells


def passed_along(block, axis, distance):
    devices = range(lax.axis_size(axis))
    route = [((i - distance) % len(devices), i) for i in devices]
    return lax.ppermute(block, axis, route)


def neighbour_tiles(row_at, col_at, lat_tiles, lon_tiles):
    row_step = jnp.array([-1, -1, -1, 0, 0, 0, 1, 1, 1], dtype=jnp.int32)
    col_step = jnp.array([-1, 0, 1, -1, 0, 1, -1, 0, 1], dtype=jnp.int32)
    row_next = row_at + row_step
    across = (row_next < 0) | (row_next > lat_tiles - 1)
    col_next = (col_at + col_step + jnp.where(across, lon_tiles // 2, 0)) % lon_tiles
    row_next = jnp.clip(row_next, 0, lat_tiles - 1)
    return row_next * lon_tiles + col_next


def close_poles(rim_block, mirror):
    lat_index = lax.axis_index("lat")
    last_index = lax.axis_size("lat") - 1
    north_rim = jnp.where(lat_index == 0, mirror, rim_block[:1])
    south_rim = jnp.where(lat_index == last_index, mirror, rim_block[-1:])
    return jnp.concatenate([north_rim, rim_block[1:-1], south_rim], 0)


def around_pair(first_block, second_block):
    row_faces = (
        with_halo(first_block, (("lat", 0),), 1, False),
        with_halo(second_block, (("lat", 0),), 1, False),
    )
    mirror = passed_along((first_block, second_block), "lon", lax.axis_size("lon") // 2)
    column_a = close_poles(row_faces[0], mirror[0])
    column_b = close_poles(row_faces[1], mirror[1])
    return (
        with_halo(column_a, (("lon", 1),), 1, True),
        with_halo(column_b, (("lon", 1),), 1, True),
    )


def around_stats(log_total, out_dot):
    near_stats = (
        with_halo(log_total, (("lon", 1), ("lat", 0)), 1, True),
        with_halo(out_dot, (("lon", 1), ("lat", 0)), 1, True),
    )
    own_rows = log_total.shape[0]
    own_total = near_stats[0][1 : own_rows + 1]
    own_dot = near_stats[1][1 : own_rows + 1]
    mirror = passed_along((own_total, own_dot), "lon", lax.axis_size("lon") // 2)
    return (close_poles(near_stats[0], mirror[0]), close_poles(near_stats[1], mirror[1]))


def on_device_general(queries, key_tokens, value_tokens, out_grad, counts):
    own_rows = queries.shape[0]
    tile_len = queries.shape[2]
    feat_width = queries.shape[3]
    head_count = feat_width // HD
    lat_tiles = counts.shape[0]
    lon_tiles = counts.shape[1]
    row_base = lax.axis_index("lat") * own_rows
    col_at = lax.axis_index("lon")
    score_scale = 1.0 / math.sqrt(HD)
    positions = jnp.arange(tile_len, dtype=jnp.int32)
    flat_counts = counts.reshape(-1)
    near_k, near_v = around_pair(key_tokens, value_tokens)
    attended_rows, query_rows, total_rows, dot_rows = ([], [], [], [])
    row_local = 0
    slot_ids = neighbour_tiles(row_base + row_local, col_at, lat_tiles, lon_tiles)
    key_valid = (positions[None, :] < flat_counts[slot_ids][:, None]).reshape(-1)
    near_keys = near_k.reshape(9 * tile_len, feat_width)
    near_values = near_v.reshape(9 * tile_len, feat_width)
    head_outs = []
    query_parts = []
    head_totals = []
    head_dots = []
    for head_index in range(head_count):
        columns = slice(head_index * HD, (head_index + 1) * HD)
        query_here = queries[row_local, 0, :, columns]
        grad_here = out_grad[row_local, 0, :, columns]
        keys_head = near_keys[:, columns]
        values_head = near_values[:, columns]
        scores = (
            jnp.einsum("qd,kd->qk", query_here, keys_head, preferred_element_type=jnp.float32)
            * score_scale
        )
        row_max = jnp.max(jnp.where(key_valid[None, :], scores, -1e30), axis=-1, keepdims=True)
        row_total = jnp.sum(
            jnp.where(key_valid[None, :], jnp.exp(scores - row_max), 0.0), axis=-1, keepdims=True
        )
        log_total = row_max + jnp.log(row_total)
        weights = jnp.where(key_valid[None, :], jnp.exp(scores - log_total), 0.0)
        weights_low = weights.astype(jnp.bfloat16)
        head_out = jnp.dot(weights_low, values_head, preferred_element_type=jnp.float32).astype(
            jnp.bfloat16
        )
        out_dot = jnp.sum(grad_here.astype(jnp.float32) * head_out.astype(jnp.float32), axis=-1)
        grad_weights = jnp.einsum(
            "qd,kd->qk", grad_here, values_head, preferred_element_type=jnp.float32
        )
        grad_scores = (weights * (grad_weights - out_dot[:, None])).astype(jnp.bfloat16)
        query_part = (
            jnp.dot(grad_scores, keys_head, preferred_element_type=jnp.float32) * score_scale
        )
        head_outs.append(head_out)
        query_parts.append(query_part.astype(jnp.bfloat16))
        head_totals.append(log_total[:, 0])
        head_dots.append(out_dot)
    attended_rows.append(jnp.concatenate(head_outs, -1))
    query_rows.append(jnp.concatenate(query_parts, -1))
    total_rows.append(jnp.stack(head_totals))
    dot_rows.append(jnp.stack(head_dots))
    attended = jnp.stack(attended_rows)[:, None]
    query_grad = jnp.stack(query_rows)[:, None]
    own_totals = jnp.stack(total_rows)[:, None]
    own_dots = jnp.stack(dot_rows)[:, None]
    near_q, near_g = around_pair(queries, out_grad)
    near_total, near_dot = around_stats(own_totals, own_dots)
    key_rows, value_rows = ([], [])
    row_local = 0
    own_valid = positions < counts[row_base + row_local, col_at]
    near_queries = near_q.reshape(9 * tile_len, feat_width)
    near_grads = near_g.reshape(9 * tile_len, feat_width)
    key_parts = []
    value_parts = []
    for head_index in range(head_count):
        columns = slice(head_index * HD, (head_index + 1) * HD)
        queries_head = near_queries[:, columns]
        grads_head = near_grads[:, columns]
        keys_here = key_tokens[row_local, 0, :, columns]
        values_here = value_tokens[row_local, 0, :, columns]
        totals_head = near_total[:, :, head_index, :].reshape(9 * tile_len)
        dots_head = near_dot[:, :, head_index, :].reshape(9 * tile_len)
        scores = (
            jnp.einsum("qd,kd->qk", queries_head, keys_here, preferred_element_type=jnp.float32)
            * score_scale
        )
        weights = jnp.where(own_valid[None, :], jnp.exp(scores - totals_head[:, None]), 0.0)
        weights_low = weights.astype(jnp.bfloat16)
        value_part = jnp.einsum(
            "qk,qd->kd", weights_low, grads_head, preferred_element_type=jnp.float32
        )
        grad_weights = jnp.einsum(
            "qd,kd->qk", grads_head, values_here, preferred_element_type=jnp.float32
        )
        grad_scores = (weights * (grad_weights - dots_head[:, None])).astype(jnp.bfloat16)
        key_part = (
            jnp.einsum("qk,qd->kd", grad_scores, queries_head, preferred_element_type=jnp.float32)
            * score_scale
        )
        key_parts.append(key_part.astype(jnp.bfloat16))
        value_parts.append(value_part.astype(jnp.bfloat16))
    key_rows.append(jnp.concatenate(key_parts, -1))
    value_rows.append(jnp.concatenate(value_parts, -1))
    key_grad = jnp.stack(key_rows)[:, None]
    value_grad = jnp.stack(value_rows)[:, None]
    return (attended, query_grad, key_grad, value_grad)


TILES = 8
COLS = 4
HEADS_HERE = 6
ARRAYS = 4


def head_owner(head_index, core):
    return jnp.where(core == 0, head_index + 1, head_index + 2 * (head_index // 3))


def head_of(tile, core):
    on_core0 = jnp.where((tile >= 1) & (tile <= 6), tile - 1, -1)
    on_core1 = jnp.where(tile <= 2, tile, jnp.where(tile >= 5, tile - 2, -1))
    return jnp.where(core == 0, on_core0, on_core1)


def place(tile):
    return {"lat": tile // COLS, "lon": tile % COLS}


def head_kernel(
    k_ref, v_ref, q_ref, g_ref, counts_ref,
    out_ref, dq_ref, dk_ref, dv_ref,
    got, made, key_sum, value_sum, bias_base,
    in_send, in_recv, out_send, out_recv,
):
    scale = 1.0 / math.sqrt(HD)
    lat = lax.axis_index("lat")
    lon = lax.axis_index("lon")
    core = lax.axis_index("head")
    here = lat * COLS + lon
    my_head = head_of(here, core)
    works = my_head >= 0
    sources = (k_ref, v_ref, q_ref, g_ref)
    results = (out_ref, dq_ref, dk_ref, dv_ref)

    barrier = pltpu.get_barrier_semaphore()
    for step in range(1, TILES):
        pl.semaphore_signal(
            barrier, inc=1, device_id=place((here + step) % TILES),
            device_id_type=pl.DeviceIdType.MESH,
        )
    pl.semaphore_wait(barrier, TILES - 1)

    def send_in(array, head_index):
        return pltpu.make_async_remote_copy(
            src_ref=sources[array].at[0, 0, :, pl.ds(head_index * HD, HD)],
            dst_ref=got.at[array, here],
            send_sem=in_send.at[array, head_index],
            recv_sem=in_recv.at[array, here],
            device_id=place(head_owner(head_index, core)),
            device_id_type=pl.DeviceIdType.MESH,
        )

    def keep_in(array, head_index):
        return pltpu.make_async_copy(
            sources[array].at[0, 0, :, pl.ds(head_index * HD, HD)],
            got.at[array, here],
            in_recv.at[array, here],
        )

    def send_out(array, tile):
        columns = pl.ds(pl.multiple_of(my_head * HD, HD), HD)
        return pltpu.make_async_remote_copy(
            src_ref=made.at[array, tile],
            dst_ref=results[array].at[0, 0, :, columns],
            send_sem=out_send.at[array, tile],
            recv_sem=out_recv.at[array, my_head],
            device_id=place(tile),
            device_id_type=pl.DeviceIdType.MESH,
        )

    def keep_out(array, tile):
        columns = pl.ds(pl.multiple_of(my_head * HD, HD), HD)
        return pltpu.make_async_copy(
            made.at[array, tile],
            results[array].at[0, 0, :, columns],
            out_recv.at[array, my_head],
        )

    def start_out(array, tile):
        @pl.when(tile != here)
        def _():
            send_out(array, tile).start()

        @pl.when(tile == here)
        def _():
            keep_out(array, tile).start()

    for array in range(ARRAYS):
        for head_index in range(HEADS_HERE):
            owner = head_owner(head_index, core)

            @pl.when(owner != here)
            def _():
                send_in(array, head_index).start()

            @pl.when(owner == here)
            def _():
                keep_in(array, head_index).start()

    def await_in(array, tile):
        pltpu.make_async_copy(
            got.at[array, tile], got.at[array, tile], in_recv.at[array, tile]
        ).wait()

    @pl.when(works)
    def _():
        lanes = lax.broadcasted_iota(jnp.int32, (1, HD), 1)
        for tile in range(TILES):
            valid = lanes < counts_ref[tile // COLS, tile % COLS]
            bias_base[:, tile * HD : (tile + 1) * HD] = jnp.where(valid, 0.0, -1e30)
        key_sum[...] = jnp.zeros_like(key_sum)
        value_sum[...] = jnp.zeros_like(value_sum)
        for array in range(2):
            for tile in range(TILES):
                await_in(array, tile)
        first_col = (lon // 2) * 2

        def query_tile(step, carry):
            row = step % 2
            col = (first_col + step // 2) % COLS
            tile = row * COLS + col
            await_in(2, tile)
            await_in(3, tile)
            queries = got[2, tile]
            grads = got[3, tile]
            keys = got[0].reshape(TILES * HD, HD)
            values = got[1].reshape(TILES * HD, HD)
            key_tile = lax.broadcasted_iota(jnp.int32, (1, TILES * HD), 1) // HD
            ahead = (key_tile % COLS - col + COLS) % COLS
            times = jnp.where(
                key_tile // COLS == row,
                jnp.where(ahead % 2 == 1, 1.0, 0.0),
                jnp.where(ahead == 2, -1e30, 0.0),
            )
            bias = bias_base[...] + times
            scores = lax.dot_general(
                queries, keys, (((1,), (1,)), ((), ())), preferred_element_type=jnp.float32
            ) * (scale * LOG2E) + bias
            row_max = jnp.max(scores, axis=-1, keepdims=True)
            raised = jnp.exp2(scores - row_max)
            row_total = jnp.sum(raised, axis=-1, keepdims=True)
            weights = raised * (1.0 / row_total)
            weights_low = weights.astype(jnp.bfloat16)
            attended = jnp.dot(
                weights_low, values, preferred_element_type=jnp.float32
            ).astype(jnp.bfloat16)
            made[0, tile] = attended
            start_out(0, tile)
            out_dot = jnp.sum(
                grads.astype(jnp.float32) * attended.astype(jnp.float32), axis=-1, keepdims=True
            )
            grad_weights = lax.dot_general(
                grads, values, (((1,), (1,)), ((), ())), preferred_element_type=jnp.float32
            )
            grad_scores = (weights * (grad_weights - out_dot)).astype(jnp.bfloat16)
            made[1, tile] = (
                jnp.dot(grad_scores, keys, preferred_element_type=jnp.float32) * scale
            ).astype(jnp.bfloat16)
            start_out(1, tile)
            value_sum[...] += lax.dot_general(
                grads, weights_low, (((0,), (0,)), ((), ())), preferred_element_type=jnp.float32
            )
            key_sum[...] += lax.dot_general(
                queries, grad_scores, (((0,), (0,)), ((), ())), preferred_element_type=jnp.float32
            )
            return carry

        lax.fori_loop(0, TILES, query_tile, 0)
        for tile in range(TILES):
            span = slice(tile * HD, (tile + 1) * HD)
            made[2, tile] = (key_sum[:, span].T * scale).astype(jnp.bfloat16)
            start_out(2, tile)
            made[3, tile] = value_sum[:, span].T.astype(jnp.bfloat16)
            start_out(3, tile)

    for array in range(ARRAYS):
        for head_index in range(HEADS_HERE):
            @pl.when(head_owner(head_index, core) != here)
            def _():
                send_in(array, head_index).wait_send()

    @pl.when(works)
    def _():
        for array in range(ARRAYS):
            for tile in range(TILES):
                @pl.when(here != tile)
                def _():
                    send_out(array, tile).wait_send()

    for array in range(ARRAYS):
        for head_index in range(HEADS_HERE):
            block = results[array].at[0, 0, :, pl.ds(head_index * HD, HD)]
            pltpu.make_async_copy(block, block, out_recv.at[array, head_index]).wait()


def on_device_heads(queries, key_tokens, value_tokens, out_grad, counts):
    shape = jax.ShapeDtypeStruct(queries.shape, queries.dtype)
    anywhere = pl.BlockSpec(memory_space=pl.ANY)
    return pl.pallas_call(
        head_kernel,
        out_shape=(shape,) * ARRAYS,
        in_specs=[anywhere] * ARRAYS + [pl.BlockSpec(memory_space=pltpu.SMEM)],
        out_specs=(anywhere,) * ARRAYS,
        scratch_shapes=[
            pltpu.VMEM((ARRAYS, TILES, HD, HD), jnp.bfloat16),
            pltpu.VMEM((ARRAYS, TILES, HD, HD), jnp.bfloat16),
            pltpu.VMEM((HD, TILES * HD), jnp.float32),
            pltpu.VMEM((HD, TILES * HD), jnp.float32),
            pltpu.VMEM((1, TILES * HD), jnp.float32),
            pltpu.SemaphoreType.DMA((ARRAYS, HEADS_HERE)),
            pltpu.SemaphoreType.DMA((ARRAYS, TILES)),
            pltpu.SemaphoreType.DMA((ARRAYS, TILES)),
            pltpu.SemaphoreType.DMA((ARRAYS, HEADS_HERE)),
        ],
        compiler_params=pltpu.CompilerParams(
            collective_id=0, has_side_effects=True, vmem_limit_bytes=32 * 1024 * 1024
        ),
    )(key_tokens, value_tokens, queries, out_grad, counts)


def on_device(queries, key_tokens, value_tokens, out_grad, counts):
    rings = (lax.axis_size("lat"), lax.axis_size("lon"))
    if rings == (TILES // COLS, COLS) and queries.shape == (1, 1, HD, HEADS_HERE * HD):
        return on_device_heads(queries, key_tokens, value_tokens, out_grad, counts)
    return on_device_general(queries, key_tokens, value_tokens, out_grad, counts)


def solution(mesh):
    placed = (
        P(("groups", "lat"), "lon", None, "head"),
        P(("groups", "lat"), "lon", None, "head"),
        P(("groups", "lat"), "lon", None, "head"),
        P(("groups", "lat"), "lon", None, "head"),
        P("groups", None),
    )
    return jax.shard_map(
        on_device,
        mesh=mesh,
        in_specs=placed,
        out_specs=(
            P(("groups", "lat"), "lon", None, "head"),
            P(("groups", "lat"), "lon", None, "head"),
            P(("groups", "lat"), "lon", None, "head"),
            P(("groups", "lat"), "lon", None, "head"),
        ),
        check_vma=False,
    )
```

```python
import math

import jax
import jax.numpy as jnp
from jax import lax
from jax.experimental import pallas as pl
from jax.experimental.pallas import tpu as pltpu
from jax.sharding import PartitionSpec as P

HD = 128
LOG2E = 1.4426950408889634


def with_halo(cells, sides, width, closed):
    for axis, dim in sides:
        count = lax.axis_size(axis)
        ends = count if closed else count - 1
        head = lax.slice_in_dim(cells, 0, width, axis=dim)
        tail = lax.slice_in_dim(cells, cells.shape[dim] - width, cells.shape[dim], axis=dim)
        cells = jnp.concatenate(
            [
                lax.ppermute(tail, axis, [(i, (i + 1) % count) for i in range(ends)]),
                cells,
                lax.ppermute(head, axis, [((i + 1) % count, i) for i in range(ends)]),
            ],
            axis=dim,
        )
    return cells


def passed_along(block, axis, distance):
    devices = range(lax.axis_size(axis))
    route = [((i - distance) % len(devices), i) for i in devices]
    return lax.ppermute(block, axis, route)


def neighbour_tiles(row_at, col_at, lat_tiles, lon_tiles):
    row_step = jnp.array([-1, -1, -1, 0, 0, 0, 1, 1, 1], dtype=jnp.int32)
    col_step = jnp.array([-1, 0, 1, -1, 0, 1, -1, 0, 1], dtype=jnp.int32)
    row_next = row_at + row_step
    across = (row_next < 0) | (row_next > lat_tiles - 1)
    col_next = (col_at + col_step + jnp.where(across, lon_tiles // 2, 0)) % lon_tiles
    row_next = jnp.clip(row_next, 0, lat_tiles - 1)
    return row_next * lon_tiles + col_next


def close_poles(rim_block, mirror):
    lat_index = lax.axis_index("lat")
    last_index = lax.axis_size("lat") - 1
    north_rim = jnp.where(lat_index == 0, mirror, rim_block[:1])
    south_rim = jnp.where(lat_index == last_index, mirror, rim_block[-1:])
    return jnp.concatenate([north_rim, rim_block[1:-1], south_rim], 0)


def around_pair(first_block, second_block):
    row_faces = (
        with_halo(first_block, (("lat", 0),), 1, False),
        with_halo(second_block, (("lat", 0),), 1, False),
    )
    mirror = passed_along((first_block, second_block), "lon", lax.axis_size("lon") // 2)
    column_a = close_poles(row_faces[0], mirror[0])
    column_b = close_poles(row_faces[1], mirror[1])
    return (
        with_halo(column_a, (("lon", 1),), 1, True),
        with_halo(column_b, (("lon", 1),), 1, True),
    )


def around_stats(log_total, out_dot):
    near_stats = (
        with_halo(log_total, (("lon", 1), ("lat", 0)), 1, True),
        with_halo(out_dot, (("lon", 1), ("lat", 0)), 1, True),
    )
    own_rows = log_total.shape[0]
    own_total = near_stats[0][1 : own_rows + 1]
    own_dot = near_stats[1][1 : own_rows + 1]
    mirror = passed_along((own_total, own_dot), "lon", lax.axis_size("lon") // 2)
    return (close_poles(near_stats[0], mirror[0]), close_poles(near_stats[1], mirror[1]))


def on_device_general(queries, key_tokens, value_tokens, out_grad, counts):
    own_rows = queries.shape[0]
    tile_len = queries.shape[2]
    feat_width = queries.shape[3]
    head_count = feat_width // HD
    lat_tiles = counts.shape[0]
    lon_tiles = counts.shape[1]
    row_base = lax.axis_index("lat") * own_rows
    col_at = lax.axis_index("lon")
    score_scale = 1.0 / math.sqrt(HD)
    positions = jnp.arange(tile_len, dtype=jnp.int32)
    flat_counts = counts.reshape(-1)
    near_k, near_v = around_pair(key_tokens, value_tokens)
    attended_rows, query_rows, total_rows, dot_rows = ([], [], [], [])
    row_local = 0
    slot_ids = neighbour_tiles(row_base + row_local, col_at, lat_tiles, lon_tiles)
    key_valid = (positions[None, :] < flat_counts[slot_ids][:, None]).reshape(-1)
    near_keys = near_k.reshape(9 * tile_len, feat_width)
    near_values = near_v.reshape(9 * tile_len, feat_width)
    head_outs = []
    query_parts = []
    head_totals = []
    head_dots = []
    for head_index in range(head_count):
        columns = slice(head_index * HD, (head_index + 1) * HD)
        query_here = queries[row_local, 0, :, columns]
        grad_here = out_grad[row_local, 0, :, columns]
        keys_head = near_keys[:, columns]
        values_head = near_values[:, columns]
        scores = (
            jnp.einsum("qd,kd->qk", query_here, keys_head, preferred_element_type=jnp.float32)
            * score_scale
        )
        row_max = jnp.max(jnp.where(key_valid[None, :], scores, -1e30), axis=-1, keepdims=True)
        row_total = jnp.sum(
            jnp.where(key_valid[None, :], jnp.exp(scores - row_max), 0.0), axis=-1, keepdims=True
        )
        log_total = row_max + jnp.log(row_total)
        weights = jnp.where(key_valid[None, :], jnp.exp(scores - log_total), 0.0)
        weights_low = weights.astype(jnp.bfloat16)
        head_out = jnp.dot(weights_low, values_head, preferred_element_type=jnp.float32).astype(
            jnp.bfloat16
        )
        out_dot = jnp.sum(grad_here.astype(jnp.float32) * head_out.astype(jnp.float32), axis=-1)
        grad_weights = jnp.einsum(
            "qd,kd->qk", grad_here, values_head, preferred_element_type=jnp.float32
        )
        grad_scores = (weights * (grad_weights - out_dot[:, None])).astype(jnp.bfloat16)
        query_part = (
            jnp.dot(grad_scores, keys_head, preferred_element_type=jnp.float32) * score_scale
        )
        head_outs.append(head_out)
        query_parts.append(query_part.astype(jnp.bfloat16))
        head_totals.append(log_total[:, 0])
        head_dots.append(out_dot)
    attended_rows.append(jnp.concatenate(head_outs, -1))
    query_rows.append(jnp.concatenate(query_parts, -1))
    total_rows.append(jnp.stack(head_totals))
    dot_rows.append(jnp.stack(head_dots))
    attended = jnp.stack(attended_rows)[:, None]
    query_grad = jnp.stack(query_rows)[:, None]
    own_totals = jnp.stack(total_rows)[:, None]
    own_dots = jnp.stack(dot_rows)[:, None]
    near_q, near_g = around_pair(queries, out_grad)
    near_total, near_dot = around_stats(own_totals, own_dots)
    key_rows, value_rows = ([], [])
    row_local = 0
    own_valid = positions < counts[row_base + row_local, col_at]
    near_queries = near_q.reshape(9 * tile_len, feat_width)
    near_grads = near_g.reshape(9 * tile_len, feat_width)
    key_parts = []
    value_parts = []
    for head_index in range(head_count):
        columns = slice(head_index * HD, (head_index + 1) * HD)
        queries_head = near_queries[:, columns]
        grads_head = near_grads[:, columns]
        keys_here = key_tokens[row_local, 0, :, columns]
        values_here = value_tokens[row_local, 0, :, columns]
        totals_head = near_total[:, :, head_index, :].reshape(9 * tile_len)
        dots_head = near_dot[:, :, head_index, :].reshape(9 * tile_len)
        scores = (
            jnp.einsum("qd,kd->qk", queries_head, keys_here, preferred_element_type=jnp.float32)
            * score_scale
        )
        weights = jnp.where(own_valid[None, :], jnp.exp(scores - totals_head[:, None]), 0.0)
        weights_low = weights.astype(jnp.bfloat16)
        value_part = jnp.einsum(
            "qk,qd->kd", weights_low, grads_head, preferred_element_type=jnp.float32
        )
        grad_weights = jnp.einsum(
            "qd,kd->qk", grads_head, values_here, preferred_element_type=jnp.float32
        )
        grad_scores = (weights * (grad_weights - dots_head[:, None])).astype(jnp.bfloat16)
        key_part = (
            jnp.einsum("qk,qd->kd", grad_scores, queries_head, preferred_element_type=jnp.float32)
            * score_scale
        )
        key_parts.append(key_part.astype(jnp.bfloat16))
        value_parts.append(value_part.astype(jnp.bfloat16))
    key_rows.append(jnp.concatenate(key_parts, -1))
    value_rows.append(jnp.concatenate(value_parts, -1))
    key_grad = jnp.stack(key_rows)[:, None]
    value_grad = jnp.stack(value_rows)[:, None]
    return (attended, query_grad, key_grad, value_grad)


TILES = 8
COLS = 4
HEADS_HERE = 6
ARRAYS = 4


def head_owner(head_index, core):
    return jnp.where(core == 0, head_index + 1, head_index + 2 * (head_index // 3))


def head_of(tile, core):
    on_core0 = jnp.where((tile >= 1) & (tile <= 6), tile - 1, -1)
    on_core1 = jnp.where(tile <= 2, tile, jnp.where(tile >= 5, tile - 2, -1))
    return jnp.where(core == 0, on_core0, on_core1)


def place(tile):
    return {"lat": tile // COLS, "lon": tile % COLS}


def head_kernel(
    k_ref, v_ref, q_ref, g_ref, counts_ref,
    out_ref, dq_ref, dk_ref, dv_ref,
    got, made, key_sum, value_sum, bias_base,
    counts_here, staged, stage_sem, in_send, in_recv, out_send, out_recv, counts_sem,
):
    scale = 1.0 / math.sqrt(HD)
    lat = lax.axis_index("lat")
    lon = lax.axis_index("lon")
    core = lax.axis_index("head")
    here = lat * COLS + lon
    my_head = head_of(here, core)
    works = my_head >= 0
    sources = (k_ref, v_ref, q_ref, g_ref)
    results = (out_ref, dq_ref, dk_ref, dv_ref)

    counts_copy = pltpu.make_async_copy(counts_ref, counts_here, counts_sem)
    counts_copy.start()
    stages = [
        pltpu.make_async_copy(sources[array].at[0, 0], staged.at[array], stage_sem.at[array])
        for array in range(ARRAYS)
    ]
    for stage in stages:
        stage.start()
    barrier = pltpu.get_barrier_semaphore()
    for step in range(1, TILES):
        pl.semaphore_signal(
            barrier, inc=1, device_id=place((here + step) % TILES),
            device_id_type=pl.DeviceIdType.MESH,
        )
    pl.semaphore_wait(barrier, TILES - 1)

    def send_in(array, head_index):
        return pltpu.make_async_remote_copy(
            src_ref=staged.at[array, :, pl.ds(head_index * HD, HD)],
            dst_ref=got.at[array, here],
            send_sem=in_send.at[array, head_index],
            recv_sem=in_recv.at[array, here],
            device_id=place(head_owner(head_index, core)),
            device_id_type=pl.DeviceIdType.MESH,
        )

    def keep_in(array, head_index):
        return pltpu.make_async_copy(
            staged.at[array, :, pl.ds(head_index * HD, HD)],
            got.at[array, here],
            in_recv.at[array, here],
        )

    def send_out(array, tile):
        columns = pl.ds(pl.multiple_of(my_head * HD, HD), HD)
        return pltpu.make_async_remote_copy(
            src_ref=made.at[array, tile],
            dst_ref=results[array].at[0, 0, :, columns],
            send_sem=out_send.at[array, tile],
            recv_sem=out_recv.at[array, my_head],
            device_id=place(tile),
            device_id_type=pl.DeviceIdType.MESH,
        )

    def keep_out(array, tile):
        columns = pl.ds(pl.multiple_of(my_head * HD, HD), HD)
        return pltpu.make_async_copy(
            made.at[array, tile],
            results[array].at[0, 0, :, columns],
            out_recv.at[array, my_head],
        )

    def start_out(array, tile):
        @pl.when(tile != here)
        def _():
            send_out(array, tile).start()

        @pl.when(tile == here)
        def _():
            keep_out(array, tile).start()

    for array in range(ARRAYS):
        stages[array].wait()
        for head_index in range(HEADS_HERE):
            owner = head_owner(head_index, core)

            @pl.when(owner != here)
            def _():
                send_in(array, head_index).start()

            @pl.when(owner == here)
            def _():
                keep_in(array, head_index).start()

    def await_in(array, tile):
        pltpu.make_async_copy(
            got.at[array, tile], got.at[array, tile], in_recv.at[array, tile]
        ).wait()

    counts_copy.wait()

    @pl.when(works)
    def _():
        lanes = lax.broadcasted_iota(jnp.int32, (1, HD), 1)
        for tile in range(TILES):
            valid = lanes < counts_here[tile // COLS, tile % COLS]
            bias_base[:, tile * HD : (tile + 1) * HD] = jnp.where(valid, 0.0, -1e30)
        key_sum[...] = jnp.zeros_like(key_sum)
        value_sum[...] = jnp.zeros_like(value_sum)
        for array in range(2):
            for tile in range(TILES):
                await_in(array, tile)
        first_col = (lon // 2) * 2

        def query_tile(step, carry):
            row = step % 2
            col = (first_col + step // 2) % COLS
            tile = row * COLS + col
            await_in(2, tile)
            await_in(3, tile)
            queries = got[2, tile]
            grads = got[3, tile]
            keys = got[0].reshape(TILES * HD, HD)
            values = got[1].reshape(TILES * HD, HD)
            key_tile = lax.broadcasted_iota(jnp.int32, (1, TILES * HD), 1) // HD
            ahead = (key_tile % COLS - col + COLS) % COLS
            times = jnp.where(
                key_tile // COLS == row,
                jnp.where(ahead % 2 == 1, 1.0, 0.0),
                jnp.where(ahead == 2, -1e30, 0.0),
            )
            bias = bias_base[...] + times
            scores = lax.dot_general(
                queries, keys, (((1,), (1,)), ((), ())), preferred_element_type=jnp.float32
            ) * (scale * LOG2E) + bias
            row_max = jnp.max(scores, axis=-1, keepdims=True)
            raised = jnp.exp2(scores - row_max)
            row_total = jnp.sum(raised, axis=-1, keepdims=True)
            weights = raised * (1.0 / row_total)
            weights_low = weights.astype(jnp.bfloat16)
            attended = jnp.dot(
                weights_low, values, preferred_element_type=jnp.float32
            ).astype(jnp.bfloat16)
            made[0, tile] = attended
            start_out(0, tile)
            out_dot = jnp.sum(
                grads.astype(jnp.float32) * attended.astype(jnp.float32), axis=-1, keepdims=True
            )
            grad_weights = lax.dot_general(
                grads, values, (((1,), (1,)), ((), ())), preferred_element_type=jnp.float32
            )
            grad_scores = (weights * (grad_weights - out_dot)).astype(jnp.bfloat16)
            made[1, tile] = (
                jnp.dot(grad_scores, keys, preferred_element_type=jnp.float32) * scale
            ).astype(jnp.bfloat16)
            start_out(1, tile)
            value_sum[...] += lax.dot_general(
                grads, weights_low, (((0,), (0,)), ((), ())), preferred_element_type=jnp.float32
            )
            key_sum[...] += lax.dot_general(
                queries, grad_scores, (((0,), (0,)), ((), ())), preferred_element_type=jnp.float32
            )
            return carry

        lax.fori_loop(0, TILES, query_tile, 0)
        for tile in range(TILES):
            span = slice(tile * HD, (tile + 1) * HD)
            made[2, tile] = (key_sum[:, span].T * scale).astype(jnp.bfloat16)
            start_out(2, tile)
            made[3, tile] = value_sum[:, span].T.astype(jnp.bfloat16)
            start_out(3, tile)

    for array in range(ARRAYS):
        for head_index in range(HEADS_HERE):
            @pl.when(head_owner(head_index, core) != here)
            def _():
                send_in(array, head_index).wait_send()

    @pl.when(works)
    def _():
        for array in range(ARRAYS):
            for tile in range(TILES):
                @pl.when(here != tile)
                def _():
                    send_out(array, tile).wait_send()

    for array in range(ARRAYS):
        for head_index in range(HEADS_HERE):
            block = results[array].at[0, 0, :, pl.ds(head_index * HD, HD)]
            pltpu.make_async_copy(block, block, out_recv.at[array, head_index]).wait()


def hand_over(*refs):
    for i in range(ARRAYS):
        refs[ARRAYS + i][...] = refs[i][...]


def on_device_heads(queries, key_tokens, value_tokens, out_grad, counts):
    shape = jax.ShapeDtypeStruct(queries.shape, queries.dtype)
    anywhere = pl.BlockSpec(memory_space=pl.ANY)
    results = pl.pallas_call(
        head_kernel,
        out_shape=(shape,) * ARRAYS,
        in_specs=[pl.BlockSpec(memory_space=pltpu.HBM)] * (ARRAYS + 1),
        out_specs=(anywhere,) * ARRAYS,
        scratch_shapes=[
            pltpu.VMEM((ARRAYS, TILES, HD, HD), jnp.bfloat16),
            pltpu.VMEM((ARRAYS, TILES, HD, HD), jnp.bfloat16),
            pltpu.VMEM((HD, TILES * HD), jnp.float32),
            pltpu.VMEM((HD, TILES * HD), jnp.float32),
            pltpu.VMEM((1, TILES * HD), jnp.float32),
            pltpu.SMEM(counts.shape, jnp.int32),
            pltpu.VMEM((ARRAYS, HD, HEADS_HERE * HD), jnp.bfloat16),
            pltpu.SemaphoreType.DMA((ARRAYS,)),
            pltpu.SemaphoreType.DMA((ARRAYS, HEADS_HERE)),
            pltpu.SemaphoreType.DMA((ARRAYS, TILES)),
            pltpu.SemaphoreType.DMA((ARRAYS, TILES)),
            pltpu.SemaphoreType.DMA((ARRAYS, HEADS_HERE)),
            pltpu.SemaphoreType.DMA,
        ],
        compiler_params=pltpu.CompilerParams(
            collective_id=0, has_side_effects=True, vmem_limit_bytes=62 * 1024 * 1024
        ),
    )(key_tokens, value_tokens, queries, out_grad, counts)
    return pl.pallas_call(
        hand_over,
        out_shape=(shape,) * ARRAYS,
        in_specs=[pl.BlockSpec(memory_space=pltpu.VMEM)] * ARRAYS,
        out_specs=(pl.BlockSpec(memory_space=pltpu.VMEM),) * ARRAYS,
        scratch_shapes=[],
        compiler_params=pltpu.CompilerParams(vmem_limit_bytes=62 * 1024 * 1024),
    )(*results)


def on_device(queries, key_tokens, value_tokens, out_grad, counts):
    rings = (lax.axis_size("lat"), lax.axis_size("lon"))
    if rings == (TILES // COLS, COLS) and queries.shape == (1, 1, HD, HEADS_HERE * HD):
        return on_device_heads(queries, key_tokens, value_tokens, out_grad, counts)
    return on_device_general(queries, key_tokens, value_tokens, out_grad, counts)


def solution(mesh):
    placed = (
        P(("groups", "lat"), "lon", None, "head"),
        P(("groups", "lat"), "lon", None, "head"),
        P(("groups", "lat"), "lon", None, "head"),
        P(("groups", "lat"), "lon", None, "head"),
        P("groups", None),
    )
    return jax.shard_map(
        on_device,
        mesh=mesh,
        in_specs=placed,
        out_specs=(
            P(("groups", "lat"), "lon", None, "head"),
            P(("groups", "lat"), "lon", None, "head"),
            P(("groups", "lat"), "lon", None, "head"),
            P(("groups", "lat"), "lon", None, "head"),
        ),
        check_vma=False,
    )
```

```python
import math

import jax
import jax.numpy as jnp
from jax import lax
from jax.experimental import pallas as pl
from jax.experimental.pallas import tpu as pltpu
from jax.sharding import PartitionSpec as P

HD = 128
LOG2E = 1.4426950408889634


def with_halo(cells, sides, width, closed):
    for axis, dim in sides:
        count = lax.axis_size(axis)
        ends = count if closed else count - 1
        head = lax.slice_in_dim(cells, 0, width, axis=dim)
        tail = lax.slice_in_dim(cells, cells.shape[dim] - width, cells.shape[dim], axis=dim)
        cells = jnp.concatenate(
            [
                lax.ppermute(tail, axis, [(i, (i + 1) % count) for i in range(ends)]),
                cells,
                lax.ppermute(head, axis, [((i + 1) % count, i) for i in range(ends)]),
            ],
            axis=dim,
        )
    return cells


def passed_along(block, axis, distance):
    devices = range(lax.axis_size(axis))
    route = [((i - distance) % len(devices), i) for i in devices]
    return lax.ppermute(block, axis, route)


def neighbour_tiles(row_at, col_at, lat_tiles, lon_tiles):
    row_step = jnp.array([-1, -1, -1, 0, 0, 0, 1, 1, 1], dtype=jnp.int32)
    col_step = jnp.array([-1, 0, 1, -1, 0, 1, -1, 0, 1], dtype=jnp.int32)
    row_next = row_at + row_step
    across = (row_next < 0) | (row_next > lat_tiles - 1)
    col_next = (col_at + col_step + jnp.where(across, lon_tiles // 2, 0)) % lon_tiles
    row_next = jnp.clip(row_next, 0, lat_tiles - 1)
    return row_next * lon_tiles + col_next


def close_poles(rim_block, mirror):
    lat_index = lax.axis_index("lat")
    last_index = lax.axis_size("lat") - 1
    north_rim = jnp.where(lat_index == 0, mirror, rim_block[:1])
    south_rim = jnp.where(lat_index == last_index, mirror, rim_block[-1:])
    return jnp.concatenate([north_rim, rim_block[1:-1], south_rim], 0)


def around_pair(first_block, second_block):
    row_faces = (
        with_halo(first_block, (("lat", 0),), 1, False),
        with_halo(second_block, (("lat", 0),), 1, False),
    )
    mirror = passed_along((first_block, second_block), "lon", lax.axis_size("lon") // 2)
    column_a = close_poles(row_faces[0], mirror[0])
    column_b = close_poles(row_faces[1], mirror[1])
    return (
        with_halo(column_a, (("lon", 1),), 1, True),
        with_halo(column_b, (("lon", 1),), 1, True),
    )


def around_stats(log_total, out_dot):
    near_stats = (
        with_halo(log_total, (("lon", 1), ("lat", 0)), 1, True),
        with_halo(out_dot, (("lon", 1), ("lat", 0)), 1, True),
    )
    own_rows = log_total.shape[0]
    own_total = near_stats[0][1 : own_rows + 1]
    own_dot = near_stats[1][1 : own_rows + 1]
    mirror = passed_along((own_total, own_dot), "lon", lax.axis_size("lon") // 2)
    return (close_poles(near_stats[0], mirror[0]), close_poles(near_stats[1], mirror[1]))


def on_device_general(queries, key_tokens, value_tokens, out_grad, counts):
    own_rows = queries.shape[0]
    tile_len = queries.shape[2]
    feat_width = queries.shape[3]
    head_count = feat_width // HD
    lat_tiles = counts.shape[0]
    lon_tiles = counts.shape[1]
    row_base = lax.axis_index("lat") * own_rows
    col_at = lax.axis_index("lon")
    score_scale = 1.0 / math.sqrt(HD)
    positions = jnp.arange(tile_len, dtype=jnp.int32)
    flat_counts = counts.reshape(-1)
    near_k, near_v = around_pair(key_tokens, value_tokens)
    attended_rows, query_rows, total_rows, dot_rows = ([], [], [], [])
    row_local = 0
    slot_ids = neighbour_tiles(row_base + row_local, col_at, lat_tiles, lon_tiles)
    key_valid = (positions[None, :] < flat_counts[slot_ids][:, None]).reshape(-1)
    near_keys = near_k.reshape(9 * tile_len, feat_width)
    near_values = near_v.reshape(9 * tile_len, feat_width)
    head_outs = []
    query_parts = []
    head_totals = []
    head_dots = []
    for head_index in range(head_count):
        columns = slice(head_index * HD, (head_index + 1) * HD)
        query_here = queries[row_local, 0, :, columns]
        grad_here = out_grad[row_local, 0, :, columns]
        keys_head = near_keys[:, columns]
        values_head = near_values[:, columns]
        scores = (
            jnp.einsum("qd,kd->qk", query_here, keys_head, preferred_element_type=jnp.float32)
            * score_scale
        )
        row_max = jnp.max(jnp.where(key_valid[None, :], scores, -1e30), axis=-1, keepdims=True)
        row_total = jnp.sum(
            jnp.where(key_valid[None, :], jnp.exp(scores - row_max), 0.0), axis=-1, keepdims=True
        )
        log_total = row_max + jnp.log(row_total)
        weights = jnp.where(key_valid[None, :], jnp.exp(scores - log_total), 0.0)
        weights_low = weights.astype(jnp.bfloat16)
        head_out = jnp.dot(weights_low, values_head, preferred_element_type=jnp.float32).astype(
            jnp.bfloat16
        )
        out_dot = jnp.sum(grad_here.astype(jnp.float32) * head_out.astype(jnp.float32), axis=-1)
        grad_weights = jnp.einsum(
            "qd,kd->qk", grad_here, values_head, preferred_element_type=jnp.float32
        )
        grad_scores = (weights * (grad_weights - out_dot[:, None])).astype(jnp.bfloat16)
        query_part = (
            jnp.dot(grad_scores, keys_head, preferred_element_type=jnp.float32) * score_scale
        )
        head_outs.append(head_out)
        query_parts.append(query_part.astype(jnp.bfloat16))
        head_totals.append(log_total[:, 0])
        head_dots.append(out_dot)
    attended_rows.append(jnp.concatenate(head_outs, -1))
    query_rows.append(jnp.concatenate(query_parts, -1))
    total_rows.append(jnp.stack(head_totals))
    dot_rows.append(jnp.stack(head_dots))
    attended = jnp.stack(attended_rows)[:, None]
    query_grad = jnp.stack(query_rows)[:, None]
    own_totals = jnp.stack(total_rows)[:, None]
    own_dots = jnp.stack(dot_rows)[:, None]
    near_q, near_g = around_pair(queries, out_grad)
    near_total, near_dot = around_stats(own_totals, own_dots)
    key_rows, value_rows = ([], [])
    row_local = 0
    own_valid = positions < counts[row_base + row_local, col_at]
    near_queries = near_q.reshape(9 * tile_len, feat_width)
    near_grads = near_g.reshape(9 * tile_len, feat_width)
    key_parts = []
    value_parts = []
    for head_index in range(head_count):
        columns = slice(head_index * HD, (head_index + 1) * HD)
        queries_head = near_queries[:, columns]
        grads_head = near_grads[:, columns]
        keys_here = key_tokens[row_local, 0, :, columns]
        values_here = value_tokens[row_local, 0, :, columns]
        totals_head = near_total[:, :, head_index, :].reshape(9 * tile_len)
        dots_head = near_dot[:, :, head_index, :].reshape(9 * tile_len)
        scores = (
            jnp.einsum("qd,kd->qk", queries_head, keys_here, preferred_element_type=jnp.float32)
            * score_scale
        )
        weights = jnp.where(own_valid[None, :], jnp.exp(scores - totals_head[:, None]), 0.0)
        weights_low = weights.astype(jnp.bfloat16)
        value_part = jnp.einsum(
            "qk,qd->kd", weights_low, grads_head, preferred_element_type=jnp.float32
        )
        grad_weights = jnp.einsum(
            "qd,kd->qk", grads_head, values_here, preferred_element_type=jnp.float32
        )
        grad_scores = (weights * (grad_weights - dots_head[:, None])).astype(jnp.bfloat16)
        key_part = (
            jnp.einsum("qk,qd->kd", grad_scores, queries_head, preferred_element_type=jnp.float32)
            * score_scale
        )
        key_parts.append(key_part.astype(jnp.bfloat16))
        value_parts.append(value_part.astype(jnp.bfloat16))
    key_rows.append(jnp.concatenate(key_parts, -1))
    value_rows.append(jnp.concatenate(value_parts, -1))
    key_grad = jnp.stack(key_rows)[:, None]
    value_grad = jnp.stack(value_rows)[:, None]
    return (attended, query_grad, key_grad, value_grad)


TILES = 8
COLS = 4
HEADS_HERE = 6
ARRAYS = 4


def head_owner(head_index, core):
    return jnp.where(core == 0, head_index + 1, head_index + 2 * (head_index // 3))


def head_of(tile, core):
    on_core0 = jnp.where((tile >= 1) & (tile <= 6), tile - 1, -1)
    on_core1 = jnp.where(tile <= 2, tile, jnp.where(tile >= 5, tile - 2, -1))
    return jnp.where(core == 0, on_core0, on_core1)


def place(tile):
    return {"lat": tile // COLS, "lon": tile % COLS}


def head_kernel(
    k_ref, v_ref, q_ref, g_ref, counts_ref,
    out_ref, dq_ref, dk_ref, dv_ref,
    got, made, key_sum, value_sum, bias_base,
    kept, counts_here, staged, stage_sem, in_send, in_recv, out_send, out_recv, counts_sem,
):
    scale = 1.0 / math.sqrt(HD)
    lat = lax.axis_index("lat")
    lon = lax.axis_index("lon")
    core = lax.axis_index("head")
    here = lat * COLS + lon
    my_head = head_of(here, core)
    works = my_head >= 0
    sources = (k_ref, v_ref, q_ref, g_ref)
    results = (out_ref, dq_ref, dk_ref, dv_ref)

    counts_copy = pltpu.make_async_copy(counts_ref, counts_here, counts_sem)
    counts_copy.start()
    stages = [
        pltpu.make_async_copy(sources[array].at[0, 0], staged.at[array], stage_sem.at[array])
        for array in range(ARRAYS)
    ]
    for stage in stages:
        stage.start()
    barrier = pltpu.get_barrier_semaphore()
    for step in range(1, TILES):
        pl.semaphore_signal(
            barrier, inc=1, device_id=place((here + step) % TILES),
            device_id_type=pl.DeviceIdType.MESH,
        )
    pl.semaphore_wait(barrier, TILES - 1)

    def send_in(array, head_index):
        return pltpu.make_async_remote_copy(
            src_ref=staged.at[array, :, pl.ds(head_index * HD, HD)],
            dst_ref=got.at[array, here],
            send_sem=in_send.at[array, head_index],
            recv_sem=in_recv.at[array, here],
            device_id=place(head_owner(head_index, core)),
            device_id_type=pl.DeviceIdType.MESH,
        )

    def keep_in(array, head_index):
        return pltpu.make_async_copy(
            staged.at[array, :, pl.ds(head_index * HD, HD)],
            got.at[array, here],
            in_recv.at[array, here],
        )

    def send_out(array, tile):
        columns = pl.ds(pl.multiple_of(my_head * HD, HD), HD)
        return pltpu.make_async_remote_copy(
            src_ref=made.at[array, tile],
            dst_ref=results[array].at[0, 0, :, columns],
            send_sem=out_send.at[array, tile],
            recv_sem=out_recv.at[array, my_head],
            device_id=place(tile),
            device_id_type=pl.DeviceIdType.MESH,
        )

    def keep_out(array, tile):
        columns = pl.ds(pl.multiple_of(my_head * HD, HD), HD)
        return pltpu.make_async_copy(
            made.at[array, tile],
            results[array].at[0, 0, :, columns],
            out_recv.at[array, my_head],
        )

    def start_out(array, tile):
        @pl.when(tile != here)
        def _():
            send_out(array, tile).start()

        @pl.when(tile == here)
        def _():
            keep_out(array, tile).start()

    for array in range(ARRAYS):
        stages[array].wait()
        for head_index in range(HEADS_HERE):
            owner = head_owner(head_index, core)

            @pl.when(owner != here)
            def _():
                send_in(array, head_index).start()

            @pl.when(owner == here)
            def _():
                keep_in(array, head_index).start()

    def await_in(array, tile):
        pltpu.make_async_copy(
            got.at[array, tile], got.at[array, tile], in_recv.at[array, tile]
        ).wait()

    counts_copy.wait()

    @pl.when(works)
    def _():
        lanes = lax.broadcasted_iota(jnp.int32, (1, HD), 1)
        for tile in range(TILES):
            valid = lanes < counts_here[tile // COLS, tile % COLS]
            bias_base[:, tile * HD : (tile + 1) * HD] = jnp.where(valid, 0.0, -1e30)
        key_sum[...] = jnp.zeros_like(key_sum)
        value_sum[...] = jnp.zeros_like(value_sum)
        for array in range(2):
            for tile in range(TILES):
                await_in(array, tile)
        first_col = (lon // 2) * 2

        def query_tile(step, carry):
            row = step % 2
            col = (first_col + step // 2) % COLS
            tile = row * COLS + col
            await_in(2, tile)
            queries = got[2, tile]
            keys = got[0].reshape(TILES * HD, HD)
            values = got[1].reshape(TILES * HD, HD)
            key_tile = lax.broadcasted_iota(jnp.int32, (1, TILES * HD), 1) // HD
            ahead = (key_tile % COLS - col + COLS) % COLS
            times = jnp.where(
                key_tile // COLS == row,
                jnp.where(ahead % 2 == 1, 1.0, 0.0),
                jnp.where(ahead == 2, -1e30, 0.0),
            )
            bias = bias_base[...] + times
            scores = lax.dot_general(
                queries, keys, (((1,), (1,)), ((), ())), preferred_element_type=jnp.float32
            ) * (scale * LOG2E) + bias
            row_max = jnp.max(scores, axis=-1, keepdims=True)
            raised = jnp.exp2(scores - row_max)
            row_total = jnp.sum(raised, axis=-1, keepdims=True)
            weights = raised * (1.0 / row_total)
            weights_low = weights.astype(jnp.bfloat16)
            attended = jnp.dot(
                weights_low, values, preferred_element_type=jnp.float32
            ).astype(jnp.bfloat16)
            kept[tile] = weights
            made[0, tile] = attended
            start_out(0, tile)
            return carry

        def query_tile_back(step, carry):
            row = step % 2
            col = (first_col + step // 2) % COLS
            tile = row * COLS + col
            await_in(3, tile)
            queries = got[2, tile]
            grads = got[3, tile]
            keys = got[0].reshape(TILES * HD, HD)
            values = got[1].reshape(TILES * HD, HD)
            weights = kept[tile]
            weights_low = weights.astype(jnp.bfloat16)
            attended = made[0, tile]
            out_dot = jnp.sum(
                grads.astype(jnp.float32) * attended.astype(jnp.float32), axis=-1, keepdims=True
            )
            grad_weights = lax.dot_general(
                grads, values, (((1,), (1,)), ((), ())), preferred_element_type=jnp.float32
            )
            grad_scores = (weights * (grad_weights - out_dot)).astype(jnp.bfloat16)
            made[1, tile] = (
                jnp.dot(grad_scores, keys, preferred_element_type=jnp.float32) * scale
            ).astype(jnp.bfloat16)
            start_out(1, tile)
            value_sum[...] += lax.dot_general(
                grads, weights_low, (((0,), (0,)), ((), ())), preferred_element_type=jnp.float32
            )
            key_sum[...] += lax.dot_general(
                queries, grad_scores, (((0,), (0,)), ((), ())), preferred_element_type=jnp.float32
            )
            return carry

        lax.fori_loop(0, TILES, query_tile, 0)
        lax.fori_loop(0, TILES, query_tile_back, 0)
        for tile in range(TILES):
            span = slice(tile * HD, (tile + 1) * HD)
            made[2, tile] = (key_sum[:, span].T * scale).astype(jnp.bfloat16)
            start_out(2, tile)
            made[3, tile] = value_sum[:, span].T.astype(jnp.bfloat16)
            start_out(3, tile)

    for array in range(ARRAYS):
        for head_index in range(HEADS_HERE):
            @pl.when(head_owner(head_index, core) != here)
            def _():
                send_in(array, head_index).wait_send()

    @pl.when(works)
    def _():
        for array in range(ARRAYS):
            for tile in range(TILES):
                @pl.when(here != tile)
                def _():
                    send_out(array, tile).wait_send()

    for array in range(ARRAYS):
        for head_index in range(HEADS_HERE):
            block = results[array].at[0, 0, :, pl.ds(head_index * HD, HD)]
            pltpu.make_async_copy(block, block, out_recv.at[array, head_index]).wait()


def hand_over(*refs):
    for i in range(ARRAYS):
        refs[ARRAYS + i][...] = refs[i][...]


def on_device_heads(queries, key_tokens, value_tokens, out_grad, counts):
    shape = jax.ShapeDtypeStruct(queries.shape, queries.dtype)
    anywhere = pl.BlockSpec(memory_space=pl.ANY)
    results = pl.pallas_call(
        head_kernel,
        out_shape=(shape,) * ARRAYS,
        in_specs=[pl.BlockSpec(memory_space=pltpu.HBM)] * (ARRAYS + 1),
        out_specs=(anywhere,) * ARRAYS,
        scratch_shapes=[
            pltpu.VMEM((ARRAYS, TILES, HD, HD), jnp.bfloat16),
            pltpu.VMEM((ARRAYS, TILES, HD, HD), jnp.bfloat16),
            pltpu.VMEM((HD, TILES * HD), jnp.float32),
            pltpu.VMEM((HD, TILES * HD), jnp.float32),
            pltpu.VMEM((1, TILES * HD), jnp.float32),
            pltpu.VMEM((TILES, HD, TILES * HD), jnp.float32),
            pltpu.SMEM(counts.shape, jnp.int32),
            pltpu.VMEM((ARRAYS, HD, HEADS_HERE * HD), jnp.bfloat16),
            pltpu.SemaphoreType.DMA((ARRAYS,)),
            pltpu.SemaphoreType.DMA((ARRAYS, HEADS_HERE)),
            pltpu.SemaphoreType.DMA((ARRAYS, TILES)),
            pltpu.SemaphoreType.DMA((ARRAYS, TILES)),
            pltpu.SemaphoreType.DMA((ARRAYS, HEADS_HERE)),
            pltpu.SemaphoreType.DMA,
        ],
        compiler_params=pltpu.CompilerParams(
            collective_id=0, has_side_effects=True, vmem_limit_bytes=62 * 1024 * 1024
        ),
    )(key_tokens, value_tokens, queries, out_grad, counts)
    return pl.pallas_call(
        hand_over,
        out_shape=(shape,) * ARRAYS,
        in_specs=[pl.BlockSpec(memory_space=pltpu.VMEM)] * ARRAYS,
        out_specs=(pl.BlockSpec(memory_space=pltpu.VMEM),) * ARRAYS,
        scratch_shapes=[],
        compiler_params=pltpu.CompilerParams(vmem_limit_bytes=62 * 1024 * 1024),
    )(*results)


def on_device(queries, key_tokens, value_tokens, out_grad, counts):
    rings = (lax.axis_size("lat"), lax.axis_size("lon"))
    if rings == (TILES // COLS, COLS) and queries.shape == (1, 1, HD, HEADS_HERE * HD):
        return on_device_heads(queries, key_tokens, value_tokens, out_grad, counts)
    return on_device_general(queries, key_tokens, value_tokens, out_grad, counts)


def solution(mesh):
    placed = (
        P(("groups", "lat"), "lon", None, "head"),
        P(("groups", "lat"), "lon", None, "head"),
        P(("groups", "lat"), "lon", None, "head"),
        P(("groups", "lat"), "lon", None, "head"),
        P("groups", None),
    )
    return jax.shard_map(
        on_device,
        mesh=mesh,
        in_specs=placed,
        out_specs=(
            P(("groups", "lat"), "lon", None, "head"),
            P(("groups", "lat"), "lon", None, "head"),
            P(("groups", "lat"), "lon", None, "head"),
            P(("groups", "lat"), "lon", None, "head"),
        ),
        check_vma=False,
    )
```

```python
import math

import jax
import jax.numpy as jnp
from jax import lax
from jax.experimental import pallas as pl
from jax.experimental.pallas import tpu as pltpu
from jax.sharding import PartitionSpec as P

HD = 128
LOG2E = 1.4426950408889634


def with_halo(cells, sides, width, closed):
    for axis, dim in sides:
        count = lax.axis_size(axis)
        ends = count if closed else count - 1
        head = lax.slice_in_dim(cells, 0, width, axis=dim)
        tail = lax.slice_in_dim(cells, cells.shape[dim] - width, cells.shape[dim], axis=dim)
        cells = jnp.concatenate(
            [
                lax.ppermute(tail, axis, [(i, (i + 1) % count) for i in range(ends)]),
                cells,
                lax.ppermute(head, axis, [((i + 1) % count, i) for i in range(ends)]),
            ],
            axis=dim,
        )
    return cells


def passed_along(block, axis, distance):
    devices = range(lax.axis_size(axis))
    route = [((i - distance) % len(devices), i) for i in devices]
    return lax.ppermute(block, axis, route)


def neighbour_tiles(row_at, col_at, lat_tiles, lon_tiles):
    row_step = jnp.array([-1, -1, -1, 0, 0, 0, 1, 1, 1], dtype=jnp.int32)
    col_step = jnp.array([-1, 0, 1, -1, 0, 1, -1, 0, 1], dtype=jnp.int32)
    row_next = row_at + row_step
    across = (row_next < 0) | (row_next > lat_tiles - 1)
    col_next = (col_at + col_step + jnp.where(across, lon_tiles // 2, 0)) % lon_tiles
    row_next = jnp.clip(row_next, 0, lat_tiles - 1)
    return row_next * lon_tiles + col_next


def close_poles(rim_block, mirror):
    lat_index = lax.axis_index("lat")
    last_index = lax.axis_size("lat") - 1
    north_rim = jnp.where(lat_index == 0, mirror, rim_block[:1])
    south_rim = jnp.where(lat_index == last_index, mirror, rim_block[-1:])
    return jnp.concatenate([north_rim, rim_block[1:-1], south_rim], 0)


def around_pair(first_block, second_block):
    row_faces = (
        with_halo(first_block, (("lat", 0),), 1, False),
        with_halo(second_block, (("lat", 0),), 1, False),
    )
    mirror = passed_along((first_block, second_block), "lon", lax.axis_size("lon") // 2)
    column_a = close_poles(row_faces[0], mirror[0])
    column_b = close_poles(row_faces[1], mirror[1])
    return (
        with_halo(column_a, (("lon", 1),), 1, True),
        with_halo(column_b, (("lon", 1),), 1, True),
    )


def around_stats(log_total, out_dot):
    near_stats = (
        with_halo(log_total, (("lon", 1), ("lat", 0)), 1, True),
        with_halo(out_dot, (("lon", 1), ("lat", 0)), 1, True),
    )
    own_rows = log_total.shape[0]
    own_total = near_stats[0][1 : own_rows + 1]
    own_dot = near_stats[1][1 : own_rows + 1]
    mirror = passed_along((own_total, own_dot), "lon", lax.axis_size("lon") // 2)
    return (close_poles(near_stats[0], mirror[0]), close_poles(near_stats[1], mirror[1]))


def on_device_general(queries, key_tokens, value_tokens, out_grad, counts):
    own_rows = queries.shape[0]
    tile_len = queries.shape[2]
    feat_width = queries.shape[3]
    head_count = feat_width // HD
    lat_tiles = counts.shape[0]
    lon_tiles = counts.shape[1]
    row_base = lax.axis_index("lat") * own_rows
    col_at = lax.axis_index("lon")
    score_scale = 1.0 / math.sqrt(HD)
    positions = jnp.arange(tile_len, dtype=jnp.int32)
    flat_counts = counts.reshape(-1)
    near_k, near_v = around_pair(key_tokens, value_tokens)
    attended_rows, query_rows, total_rows, dot_rows = ([], [], [], [])
    row_local = 0
    slot_ids = neighbour_tiles(row_base + row_local, col_at, lat_tiles, lon_tiles)
    key_valid = (positions[None, :] < flat_counts[slot_ids][:, None]).reshape(-1)
    near_keys = near_k.reshape(9 * tile_len, feat_width)
    near_values = near_v.reshape(9 * tile_len, feat_width)
    head_outs = []
    query_parts = []
    head_totals = []
    head_dots = []
    for head_index in range(head_count):
        columns = slice(head_index * HD, (head_index + 1) * HD)
        query_here = queries[row_local, 0, :, columns]
        grad_here = out_grad[row_local, 0, :, columns]
        keys_head = near_keys[:, columns]
        values_head = near_values[:, columns]
        scores = (
            jnp.einsum("qd,kd->qk", query_here, keys_head, preferred_element_type=jnp.float32)
            * score_scale
        )
        row_max = jnp.max(jnp.where(key_valid[None, :], scores, -1e30), axis=-1, keepdims=True)
        row_total = jnp.sum(
            jnp.where(key_valid[None, :], jnp.exp(scores - row_max), 0.0), axis=-1, keepdims=True
        )
        log_total = row_max + jnp.log(row_total)
        weights = jnp.where(key_valid[None, :], jnp.exp(scores - log_total), 0.0)
        weights_low = weights.astype(jnp.bfloat16)
        head_out = jnp.dot(weights_low, values_head, preferred_element_type=jnp.float32).astype(
            jnp.bfloat16
        )
        out_dot = jnp.sum(grad_here.astype(jnp.float32) * head_out.astype(jnp.float32), axis=-1)
        grad_weights = jnp.einsum(
            "qd,kd->qk", grad_here, values_head, preferred_element_type=jnp.float32
        )
        grad_scores = (weights * (grad_weights - out_dot[:, None])).astype(jnp.bfloat16)
        query_part = (
            jnp.dot(grad_scores, keys_head, preferred_element_type=jnp.float32) * score_scale
        )
        head_outs.append(head_out)
        query_parts.append(query_part.astype(jnp.bfloat16))
        head_totals.append(log_total[:, 0])
        head_dots.append(out_dot)
    attended_rows.append(jnp.concatenate(head_outs, -1))
    query_rows.append(jnp.concatenate(query_parts, -1))
    total_rows.append(jnp.stack(head_totals))
    dot_rows.append(jnp.stack(head_dots))
    attended = jnp.stack(attended_rows)[:, None]
    query_grad = jnp.stack(query_rows)[:, None]
    own_totals = jnp.stack(total_rows)[:, None]
    own_dots = jnp.stack(dot_rows)[:, None]
    near_q, near_g = around_pair(queries, out_grad)
    near_total, near_dot = around_stats(own_totals, own_dots)
    key_rows, value_rows = ([], [])
    row_local = 0
    own_valid = positions < counts[row_base + row_local, col_at]
    near_queries = near_q.reshape(9 * tile_len, feat_width)
    near_grads = near_g.reshape(9 * tile_len, feat_width)
    key_parts = []
    value_parts = []
    for head_index in range(head_count):
        columns = slice(head_index * HD, (head_index + 1) * HD)
        queries_head = near_queries[:, columns]
        grads_head = near_grads[:, columns]
        keys_here = key_tokens[row_local, 0, :, columns]
        values_here = value_tokens[row_local, 0, :, columns]
        totals_head = near_total[:, :, head_index, :].reshape(9 * tile_len)
        dots_head = near_dot[:, :, head_index, :].reshape(9 * tile_len)
        scores = (
            jnp.einsum("qd,kd->qk", queries_head, keys_here, preferred_element_type=jnp.float32)
            * score_scale
        )
        weights = jnp.where(own_valid[None, :], jnp.exp(scores - totals_head[:, None]), 0.0)
        weights_low = weights.astype(jnp.bfloat16)
        value_part = jnp.einsum(
            "qk,qd->kd", weights_low, grads_head, preferred_element_type=jnp.float32
        )
        grad_weights = jnp.einsum(
            "qd,kd->qk", grads_head, values_here, preferred_element_type=jnp.float32
        )
        grad_scores = (weights * (grad_weights - dots_head[:, None])).astype(jnp.bfloat16)
        key_part = (
            jnp.einsum("qk,qd->kd", grad_scores, queries_head, preferred_element_type=jnp.float32)
            * score_scale
        )
        key_parts.append(key_part.astype(jnp.bfloat16))
        value_parts.append(value_part.astype(jnp.bfloat16))
    key_rows.append(jnp.concatenate(key_parts, -1))
    value_rows.append(jnp.concatenate(value_parts, -1))
    key_grad = jnp.stack(key_rows)[:, None]
    value_grad = jnp.stack(value_rows)[:, None]
    return (attended, query_grad, key_grad, value_grad)


TILES = 8
COLS = 4
HEADS_HERE = 6
ARRAYS = 4


def head_owner(head_index, core):
    return jnp.where(core == 0, head_index + 1, head_index + 2 * (head_index // 3))


def head_of(tile, core):
    on_core0 = jnp.where((tile >= 1) & (tile <= 6), tile - 1, -1)
    on_core1 = jnp.where(tile <= 2, tile, jnp.where(tile >= 5, tile - 2, -1))
    return jnp.where(core == 0, on_core0, on_core1)


def place(tile):
    return {"lat": tile // COLS, "lon": tile % COLS}


def head_kernel(
    k_ref, v_ref, q_ref, g_ref, counts_ref,
    out_ref, dq_ref, dk_ref, dv_ref,
    got, made, key_sum, value_sum, bias_base,
    kept, counts_here, staged, stage_sem, in_send, in_recv, out_send, out_recv, counts_sem,
):
    scale = 1.0 / math.sqrt(HD)
    lat = lax.axis_index("lat")
    lon = lax.axis_index("lon")
    core = lax.axis_index("head")
    here = lat * COLS + lon
    my_head = head_of(here, core)
    works = my_head >= 0
    sources = (k_ref, v_ref, q_ref, g_ref)
    results = (out_ref, dq_ref, dk_ref, dv_ref)

    counts_copy = pltpu.make_async_copy(counts_ref, counts_here, counts_sem)
    counts_copy.start()
    stages = [
        pltpu.make_async_copy(sources[array].at[0, 0], staged.at[array], stage_sem.at[array])
        for array in range(ARRAYS)
    ]
    for stage in stages:
        stage.start()
    barrier = pltpu.get_barrier_semaphore()
    for step in range(1, TILES):
        pl.semaphore_signal(
            barrier, inc=1, device_id=place((here + step) % TILES),
            device_id_type=pl.DeviceIdType.MESH,
        )
    pl.semaphore_wait(barrier, TILES - 1)

    def send_in(array, head_index):
        return pltpu.make_async_remote_copy(
            src_ref=staged.at[array, :, pl.ds(head_index * HD, HD)],
            dst_ref=got.at[array, here],
            send_sem=in_send.at[array, head_index],
            recv_sem=in_recv.at[array, here],
            device_id=place(head_owner(head_index, core)),
            device_id_type=pl.DeviceIdType.MESH,
        )

    def keep_in(array, head_index):
        return pltpu.make_async_copy(
            staged.at[array, :, pl.ds(head_index * HD, HD)],
            got.at[array, here],
            in_recv.at[array, here],
        )

    def send_out(array, tile):
        columns = pl.ds(pl.multiple_of(my_head * HD, HD), HD)
        return pltpu.make_async_remote_copy(
            src_ref=made.at[array, tile],
            dst_ref=results[array].at[0, 0, :, columns],
            send_sem=out_send.at[array, tile],
            recv_sem=out_recv.at[array, my_head],
            device_id=place(tile),
            device_id_type=pl.DeviceIdType.MESH,
        )

    def keep_out(array, tile):
        columns = pl.ds(pl.multiple_of(my_head * HD, HD), HD)
        return pltpu.make_async_copy(
            made.at[array, tile],
            results[array].at[0, 0, :, columns],
            out_recv.at[array, my_head],
        )

    def start_out(array, tile):
        @pl.when(tile != here)
        def _():
            send_out(array, tile).start()

        @pl.when(tile == here)
        def _():
            keep_out(array, tile).start()

    for array in range(ARRAYS):
        stages[array].wait()
        for head_index in range(HEADS_HERE):
            owner = head_owner(head_index, core)

            @pl.when(owner != here)
            def _():
                send_in(array, head_index).start()

            @pl.when(owner == here)
            def _():
                keep_in(array, head_index).start()

    def await_in(array, tile):
        pltpu.make_async_copy(
            got.at[array, tile], got.at[array, tile], in_recv.at[array, tile]
        ).wait()

    counts_copy.wait()

    @pl.when(works)
    def _():
        lanes = lax.broadcasted_iota(jnp.int32, (1, HD), 1)
        for tile in range(TILES):
            valid = lanes < counts_here[tile // COLS, tile % COLS]
            bias_base[:, tile * HD : (tile + 1) * HD] = jnp.where(valid, 0.0, -1e30)
        key_sum[...] = jnp.zeros_like(key_sum)
        value_sum[...] = jnp.zeros_like(value_sum)
        for array in range(2):
            for tile in range(TILES):
                await_in(array, tile)
        first_col = (lon // 2) * 2

        def query_tile(step, carry):
            row = step % 2
            col = (first_col + step // 2) % COLS
            tile = row * COLS + col
            await_in(2, tile)
            queries = got[2, tile]
            keys = got[0].reshape(TILES * HD, HD)
            values = got[1].reshape(TILES * HD, HD)
            key_tile = lax.broadcasted_iota(jnp.int32, (1, TILES * HD), 1) // HD
            ahead = (key_tile % COLS - col + COLS) % COLS
            times = jnp.where(
                key_tile // COLS == row,
                jnp.where(ahead % 2 == 1, 1.0, 0.0),
                jnp.where(ahead == 2, -1e30, 0.0),
            )
            bias = bias_base[...] + times
            scores = lax.dot_general(
                queries, keys, (((1,), (1,)), ((), ())), preferred_element_type=jnp.float32
            ) * (scale * LOG2E) + bias
            row_max = jnp.max(scores, axis=-1, keepdims=True)
            raised = jnp.exp2(scores - row_max)
            row_total = jnp.sum(raised, axis=-1, keepdims=True)
            weights = raised * (1.0 / row_total)
            weights_low = weights.astype(jnp.bfloat16)
            attended = jnp.dot(
                weights_low, values, preferred_element_type=jnp.float32
            ).astype(jnp.bfloat16)
            kept[tile] = weights
            made[0, tile] = attended
            start_out(0, tile)
            return carry

        def query_tile_back(step, carry):
            row = step % 2
            col = (first_col + step // 2) % COLS
            tile = row * COLS + col
            await_in(3, tile)
            queries = got[2, tile]
            grads = got[3, tile]
            keys = got[0].reshape(TILES * HD, HD)
            values = got[1].reshape(TILES * HD, HD)
            weights = kept[tile]
            weights_low = weights.astype(jnp.bfloat16)
            attended = made[0, tile]
            out_dot = jnp.sum(
                grads.astype(jnp.float32) * attended.astype(jnp.float32), axis=-1, keepdims=True
            )
            grad_weights = lax.dot_general(
                grads, values, (((1,), (1,)), ((), ())), preferred_element_type=jnp.float32
            )
            grad_scores = (weights * (grad_weights - out_dot)).astype(jnp.bfloat16)
            made[1, tile] = (
                jnp.dot(grad_scores, keys, preferred_element_type=jnp.float32) * scale
            ).astype(jnp.bfloat16)
            start_out(1, tile)
            value_sum[...] += lax.dot_general(
                grads, weights_low, (((0,), (0,)), ((), ())), preferred_element_type=jnp.float32
            )
            key_sum[...] += lax.dot_general(
                queries, grad_scores, (((0,), (0,)), ((), ())), preferred_element_type=jnp.float32
            )
            return carry

        lax.fori_loop(0, TILES, query_tile, 0, unroll=2)
        lax.fori_loop(0, TILES, query_tile_back, 0, unroll=2)
        for tile in range(TILES):
            span = slice(tile * HD, (tile + 1) * HD)
            made[2, tile] = (key_sum[:, span].T * scale).astype(jnp.bfloat16)
            start_out(2, tile)
            made[3, tile] = value_sum[:, span].T.astype(jnp.bfloat16)
            start_out(3, tile)

    for array in range(ARRAYS):
        for head_index in range(HEADS_HERE):
            @pl.when(head_owner(head_index, core) != here)
            def _():
                send_in(array, head_index).wait_send()

    @pl.when(works)
    def _():
        for array in range(ARRAYS):
            for tile in range(TILES):
                @pl.when(here != tile)
                def _():
                    send_out(array, tile).wait_send()

    for array in range(ARRAYS):
        for head_index in range(HEADS_HERE):
            block = results[array].at[0, 0, :, pl.ds(head_index * HD, HD)]
            pltpu.make_async_copy(block, block, out_recv.at[array, head_index]).wait()


def hand_over(*refs):
    halves, sems = refs[2 * ARRAYS], refs[2 * ARRAYS + 1]
    loads = [pltpu.make_async_copy(refs[i], halves.at[i], sems.at[0, i]) for i in range(ARRAYS)]
    saves = [
        pltpu.make_async_copy(halves.at[i], refs[ARRAYS + i], sems.at[1, i]) for i in range(ARRAYS)
    ]
    for load in loads:
        load.start()
    for load, save in zip(loads, saves):
        load.wait()
        save.start()
    for save in saves:
        save.wait()


def on_device_heads(queries, key_tokens, value_tokens, out_grad, counts):
    shape = jax.ShapeDtypeStruct(queries.shape, queries.dtype)
    anywhere = pl.BlockSpec(memory_space=pl.ANY)
    results = pl.pallas_call(
        head_kernel,
        out_shape=(shape,) * ARRAYS,
        in_specs=[pl.BlockSpec(memory_space=pltpu.HBM)] * (ARRAYS + 1),
        out_specs=(anywhere,) * ARRAYS,
        scratch_shapes=[
            pltpu.VMEM((ARRAYS, TILES, HD, HD), jnp.bfloat16),
            pltpu.VMEM((ARRAYS, TILES, HD, HD), jnp.bfloat16),
            pltpu.VMEM((HD, TILES * HD), jnp.float32),
            pltpu.VMEM((HD, TILES * HD), jnp.float32),
            pltpu.VMEM((1, TILES * HD), jnp.float32),
            pltpu.VMEM((TILES, HD, TILES * HD), jnp.float32),
            pltpu.SMEM(counts.shape, jnp.int32),
            pltpu.VMEM((ARRAYS, HD, HEADS_HERE * HD), jnp.bfloat16),
            pltpu.SemaphoreType.DMA((ARRAYS,)),
            pltpu.SemaphoreType.DMA((ARRAYS, HEADS_HERE)),
            pltpu.SemaphoreType.DMA((ARRAYS, TILES)),
            pltpu.SemaphoreType.DMA((ARRAYS, TILES)),
            pltpu.SemaphoreType.DMA((ARRAYS, HEADS_HERE)),
            pltpu.SemaphoreType.DMA,
        ],
        compiler_params=pltpu.CompilerParams(
            collective_id=0, has_side_effects=True, vmem_limit_bytes=62 * 1024 * 1024
        ),
    )(key_tokens, value_tokens, queries, out_grad, counts)
    return pl.pallas_call(
        hand_over,
        out_shape=(shape,) * ARRAYS,
        in_specs=[pl.BlockSpec(memory_space=pltpu.HBM)] * ARRAYS,
        out_specs=(pl.BlockSpec(memory_space=pltpu.HBM),) * ARRAYS,
        scratch_shapes=[pltpu.VMEM((ARRAYS,) + queries.shape, queries.dtype), pltpu.SemaphoreType.DMA((2, ARRAYS))],
        compiler_params=pltpu.CompilerParams(vmem_limit_bytes=62 * 1024 * 1024),
    )(*results)


def on_device(queries, key_tokens, value_tokens, out_grad, counts):
    rings = (lax.axis_size("lat"), lax.axis_size("lon"))
    if rings == (TILES // COLS, COLS) and queries.shape == (1, 1, HD, HEADS_HERE * HD):
        return on_device_heads(queries, key_tokens, value_tokens, out_grad, counts)
    return on_device_general(queries, key_tokens, value_tokens, out_grad, counts)


def solution(mesh):
    placed = (
        P(("groups", "lat"), "lon", None, "head"),
        P(("groups", "lat"), "lon", None, "head"),
        P(("groups", "lat"), "lon", None, "head"),
        P(("groups", "lat"), "lon", None, "head"),
        P("groups", None),
    )
    return jax.shard_map(
        on_device,
        mesh=mesh,
        in_specs=placed,
        out_specs=(
            P(("groups", "lat"), "lon", None, "head"),
            P(("groups", "lat"), "lon", None, "head"),
            P(("groups", "lat"), "lon", None, "head"),
            P(("groups", "lat"), "lon", None, "head"),
        ),
        check_vma=False,
    )
```
